32 devices in a mesh: layer: 2 (over core), row: 4 (over z), rep: 4 (over y, x).
Axes of the slice: x: 2, y: 2, z: 4, core: 2. Of those that a mesh axis runs over, the one named last changes fastest.
Arguments:
- features: bfloat16 [2048, 256], P(('row', 'rep')), may hold values from -6 to 6
- class_ids: int32 [2048], P(('row', 'rep')), may hold values from 0 to 256
- label_table: bfloat16 [256, 256], replicated, may hold values from -3 to 3
- self_weight: bfloat16 [2, 256, 256], P('layer'), may hold values from -0.375 to 0.375
- neighbor_weight: bfloat16 [2, 256, 256], P('layer'), may hold values from -0.375 to 0.375
- norm_scale: float32 [256], replicated, may hold values from 0.1 to 1.9
- tile_values: bfloat16 [4, 4, 32, 128, 128], P('row', 'rep')
- tile_block_row: int32 [4, 4, 32], P('row', 'rep'), may hold values from 0 to 3, as said below
- tile_section: int32 [4, 4, 32], P('row', 'rep'), may hold values from 0 to 3
- tile_count: int32 [4, 4], P('row', 'rep'), may hold values from 4 to 32, as said below
Outputs:
- hidden_states: bfloat16 [2, 2048, 256], P('layer', ('row', 'rep'))
The draws below stay inside these ranges and needn't reach their ends.
Inputs may be any that keep to these rules, and one draw needn't show every extreme that they name: `class_ids`: 256 marks a node without a label. `tile_block_row`: slots 0 to 3 of every device name block rows 0 to 3 in order. `tile_count`: at least 4; 32 on some device.
All inputs are finite; a program needn't handle non-finite values.
Results may differ from the reference program's by a relative error of at most 0.0052.
Values may be sent and summed in bfloat16 or wider, within the bound.
No kernel may reach another device: no remote copies, remote signals or barrier semaphores. Data moves between devices by JAX's collectives and lax.ppermute only.
A program may use at most 64 MiB of HBM per device.

```python
import math
import jax
import jax.numpy as jnp
from jax import lax

F = 256
CLASSES = 256
BLOCK = 128
K_DEV = 32
GROUPS = 4
SPLITS = 4
NODES = 2048


def draw_tile_values(key, part):
    first_key, second_key = jax.random.split(key)
    shape = (GROUPS, SPLITS, K_DEV, BLOCK, BLOCK)
    row_scale = jnp.exp(jax.random.uniform(first_key, (GROUPS, SPLITS, K_DEV, BLOCK, 1), jnp.float32, math.log(0.1), 0.0))
    entries = jnp.exp(jax.random.uniform(second_key, shape, jnp.float32, math.log(0.05), 0.0))
    return (entries * row_scale).astype(jnp.bfloat16)


def draw_tile_block_row(key, part):
    drawn = jax.random.randint(key, (GROUPS, SPLITS, K_DEV), 0, SPLITS)
    slot_ids = jnp.arange(K_DEV, dtype=jnp.int32)
    return jnp.where(slot_ids[None, None, :] < SPLITS, slot_ids[None, None, :], drawn).astype(jnp.int32)


def draw_tile_count(key, part):
    first_key, second_key = jax.random.split(key)
    counts = jax.random.randint(first_key, (GROUPS * SPLITS,), SPLITS, K_DEV + 1)
    chosen = jax.random.randint(second_key, (), 0, GROUPS * SPLITS)
    flat = jnp.where(jnp.arange(GROUPS * SPLITS, dtype=jnp.int32) == chosen, K_DEV, counts)
    return flat.reshape(GROUPS, SPLITS).astype(jnp.int32)


def set_ends(values, key, low, largest):
    index_at = [jax.random.randint(jax.random.fold_in(key, axis), (), 0, length) for axis, length in enumerate(values.shape)]
    widest = values.shape.index(max(values.shape))
    neighbour = index_at[:widest] + [(index_at[widest] + 1) % values.shape[widest]] + index_at[widest + 1:]
    return values.at[tuple(index_at)].set(low).at[tuple(neighbour)].set(largest)


def levels(rng, dims, shards, smallest, largest):
    def one(axis_at, shards_of):
        steps = jax.random.uniform(jax.random.fold_in(jax.random.fold_in(rng, 6), axis_at), (shards_of,), jnp.float32, smallest / len(shards), largest / len(shards))
        return jnp.repeat(jnp.exp(steps), dims[axis_at] // shards_of).reshape((-1,) + (1,) * (len(dims) - axis_at - 1))

    level = one(*shards[0])
    for cut in shards[1:]:
        level = level * one(*cut)
    return level


def normal_values(stream_key, dims, width, most, cuts=(), kind=jnp.bfloat16):
    values = width * jax.random.normal(stream_key, dims, jnp.float32)
    if cuts:
        values = values * levels(stream_key, dims, cuts, -0.22, 0.18)
    return jnp.clip(values, -most, most).astype(kind)


def setup_inputs(seed: int = 0) -> dict:
    arg_keys = jax.random.split(jax.random.key(seed), 11)
    features = normal_values(arg_keys[0], (NODES, F), 1.0, 6.0, ((0, 16),))
    class_ids = set_ends(jax.random.randint(arg_keys[1], (NODES,), 0, CLASSES + 1), jax.random.fold_in(arg_keys[1], 1), 0, CLASSES).astype(jnp.int32)
    label_table = normal_values(arg_keys[2], (CLASSES, F), 0.5, 3.0)
    self_weight = normal_values(arg_keys[3], (2, F, F), F ** -0.5, 0.375, ((0, 2),))
    neighbor_weight = normal_values(arg_keys[4], (2, F, F), F ** -0.5, 0.375, ((0, 2),))
    norm_scale = jnp.clip(1.0 + 0.18 * jax.random.normal(arg_keys[5], (F,), jnp.float32), 0.1, 1.9)
    tile_values = draw_tile_values(jax.random.fold_in(arg_keys[10], 71), 0)
    tile_block_row = draw_tile_block_row(jax.random.fold_in(arg_keys[10], 71), 0)
    tile_section = set_ends(jax.random.randint(arg_keys[8], (GROUPS, SPLITS, K_DEV), 0, GROUPS), jax.random.fold_in(arg_keys[8], 1), 0, GROUPS - 1).astype(jnp.int32)
    tile_count = draw_tile_count(jax.random.fold_in(arg_keys[10], 71), 0)
    return {"features": features, "class_ids": class_ids, "label_table": label_table, "self_weight": self_weight, "neighbor_weight": neighbor_weight, "norm_scale": norm_scale, "tile_values": tile_values, "tile_block_row": tile_block_row, "tile_section": tile_section, "tile_count": tile_count}


def aggregate(current, tile_values, tile_block_row, tile_section, tile_count):
    groups, splits, slot_total = tile_section.shape
    tile_edge = tile_values.shape[-1]
    hidden_dim = current.shape[1]
    blocked = current.astype(jnp.float32).reshape(groups, splits, tile_edge, hidden_dim)
    slot_ids = jnp.arange(slot_total, dtype=jnp.int32)
    targets = jnp.arange(splits, dtype=jnp.int32)

    def one_group(pieces):
        tile_data, tile_rows, tile_cols, filled = pieces
        running = jnp.zeros((splits, tile_edge, hidden_dim), jnp.float32)
        degree = jnp.zeros((splits, tile_edge), jnp.float32)
        for split_no in range(splits):
            live = (slot_ids < filled[split_no]).astype(jnp.float32)
            sources = blocked[tile_cols[split_no], split_no]
            entries = tile_data[split_no].astype(jnp.float32)
            products = jnp.einsum('kab,kbf->kaf', entries, sources, precision=lax.Precision.HIGHEST)
            onto_rows = (tile_rows[split_no][None, :] == targets[:, None]).astype(jnp.float32) * live[None, :]
            running = running + jnp.einsum('sk,kaf->saf', onto_rows, products, precision=lax.Precision.HIGHEST)
            degree = degree + jnp.einsum('sk,ka->sa', onto_rows, lax.optimization_barrier(jnp.sum(entries, axis=-1)), precision=lax.Precision.HIGHEST)
        return (running.reshape(splits * tile_edge, hidden_dim), degree.reshape(splits * tile_edge))
    totals, degrees = lax.map(one_group, (tile_values, tile_block_row, tile_section, tile_count))
    return (totals.reshape(-1, hidden_dim), degrees.reshape(-1))

def settle_norm(mixture, norm_scale):
    active = jnp.maximum(mixture, 0.0)
    center = active - lax.optimization_barrier(jnp.mean(active, axis=-1, keepdims=True))
    spread = lax.optimization_barrier(jnp.mean(center * center, axis=-1, keepdims=True))
    return (center * lax.rsqrt(spread + 1e-05) * norm_scale).astype(jnp.bfloat16)

def reference(features, class_ids, label_table, self_weight, neighbor_weight, norm_scale, tile_values, tile_block_row, tile_section, tile_count):
    classes = label_table.shape[0]
    one_hot = (class_ids[:, None] == jnp.arange(classes, dtype=jnp.int32)[None, :]).astype(jnp.bfloat16)
    inputs = (features.astype(jnp.float32) + jnp.dot(one_hot, label_table, preferred_element_type=jnp.float32)).astype(jnp.bfloat16)
    summed, degree = aggregate(inputs, tile_values, tile_block_row, tile_section, tile_count)
    neighbor = (summed * lax.rsqrt(degree)[:, None]).astype(jnp.bfloat16)
    mixture = jnp.dot(inputs, self_weight[0], preferred_element_type=jnp.float32) + jnp.dot(neighbor, neighbor_weight[0], preferred_element_type=jnp.float32)
    first = settle_norm(mixture, norm_scale)
    summed_two, degree_two = aggregate(first, tile_values, tile_block_row, tile_section, tile_count)
    neighbor_two = (summed_two * lax.rsqrt(degree)[:, None]).astype(jnp.bfloat16)
    mixture_two = jnp.dot(first, self_weight[1], preferred_element_type=jnp.float32) + jnp.dot(neighbor_two, neighbor_weight[1], preferred_element_type=jnp.float32)
    logits = mixture_two.astype(jnp.bfloat16)
    return jnp.stack([first, logits])
```

```python
import functools

import jax
import jax.numpy as jnp
from jax import lax
from jax.experimental import pallas as pl
from jax.experimental.pallas import tpu as pltpu
from jax.sharding import PartitionSpec as P

AXES = ("layer", "row", "rep")
DIRECT = 8
CHUNK = 4
PAD = 16

VMEM = pl.BlockSpec(memory_space=pltpu.VMEM)
SMEM = pl.BlockSpec(memory_space=pltpu.SMEM)
BF16 = jnp.bfloat16
F32 = jnp.float32


def dot(a, b, dims=((1,), (0,))):
    return lax.dot_general(a, b, (dims, ((), ())), preferred_element_type=F32)


def split(value):
    high = value.astype(BF16)
    return high, (value - high.astype(F32)).astype(BF16)


def embed_kernel(ids, features, table, x):
    classes, nodes = table.shape[0], features.shape[0]
    hot = (lax.broadcasted_iota(jnp.int32, (classes, nodes), 0) == ids[...]).astype(BF16)
    x[...] = (features[...].astype(F32) + dot(hot, table[...], ((0,), (0,)))).astype(BF16)


def build_kernel(direct, block_rows, sections, count, tiles, x, weight, adjacency, degrees, own, total):
    row = lax.axis_index("row") if direct else 0
    rep = lax.axis_index("rep")
    edge = tiles.shape[1]
    splits = degrees.shape[0]
    total[...] = jnp.zeros_like(total)

    def add(slot, carry):
        section = jnp.bitwise_xor(sections[slot], row)
        start = pl.multiple_of(jnp.bitwise_xor(block_rows[slot], rep) * edge, edge)
        total[section, pl.ds(start, edge), :] += tiles[slot].astype(F32)
        return carry

    lax.fori_loop(0, count[0], add, 0)
    chunks, rows, width = adjacency.shape
    per = width // edge
    ones = jnp.ones((PAD, width), BF16)

    def emit(chunk, sums):
        for part in range(per):
            adjacency[chunk, :, part * edge : (part + 1) * edge] = total[chunk * per + part].astype(BF16)
        return sums + dot(ones, adjacency[chunk], ((1,), (1,)))

    sums = jnp.zeros((PAD, rows), F32)
    if chunks == 1:
        sums = emit(0, sums)
    else:
        sums = lax.fori_loop(0, chunks, emit, sums)
    for step in range(splits):
        high, low = split(sums[:, step * edge : (step + 1) * edge])
        degrees[step, :, :edge] = high
        degrees[step, :, edge : 2 * edge] = low
    nodes = x.shape[0]
    high, low = split(dot(x[...], weight[...]))
    own[:nodes] = high
    own[nodes:] = low


def spread(adjacency, blocks, total):
    if len(blocks) > 1:
        return dot(adjacency[0], jnp.concatenate([block[...] for block in blocks], axis=0))
    chunks, _, width = adjacency.shape
    total[...] = jnp.zeros_like(total)

    def add(chunk, carry):
        start = pl.multiple_of(chunk * width, width)
        total[...] += dot(adjacency[chunk], blocks[0][pl.ds(start, width), :])
        return carry

    lax.fori_loop(0, chunks, add, 0)
    return total[...]


def first_kernel(count, *refs):
    blocks, (adjacency, degrees, own, weight) = refs[:count], refs[count : count + 4]
    sent, total = refs[count + 4 : -1], refs[-1]
    nodes = sent[1].shape[0] - PAD
    partial = spread(adjacency, blocks, total).astype(BF16)
    mixed = dot(partial, weight[...]).astype(BF16)
    for step, out in enumerate(sent):
        out[:nodes] = mixed[step * nodes : (step + 1) * nodes]
        out[nodes : nodes + PAD] = degrees[step]
    sent[0][nodes + PAD :] = own[...]


def norm_kernel(count, *refs):
    got, norm_scale = refs[:count], refs[count]
    hidden, scale = refs[count + 1 :]
    nodes = hidden.shape[0]
    value = got[0][:nodes].astype(F32)
    degree = got[0][nodes : nodes + PAD].astype(F32)
    for part in got[1:]:
        value += part[:nodes].astype(F32)
        degree += part[nodes : nodes + PAD].astype(F32)
    degree = degree[:1, :nodes] + degree[:1, nodes : 2 * nodes]
    diagonal = lax.broadcasted_iota(jnp.int32, (nodes, nodes), 0) == lax.broadcasted_iota(
        jnp.int32, (nodes, nodes), 1
    )
    inverse = jnp.sum(jnp.where(diagonal, lax.rsqrt(degree), 0.0), axis=1, keepdims=True)
    scale[...] = jnp.broadcast_to(inverse, scale.shape)
    own = got[0][nodes + PAD : 2 * nodes + PAD].astype(F32) + got[0][2 * nodes + PAD :].astype(F32)
    active = jnp.maximum(own + value * inverse, 0.0)
    center = active - jnp.mean(active, axis=-1, keepdims=True)
    spread_of = jnp.mean(center * center, axis=-1, keepdims=True)
    hidden[...] = (center * lax.rsqrt(spread_of + 1e-05) * norm_scale[...]).astype(BF16)


def second_kernel(count, *refs):
    blocks, (adjacency, hidden, weight) = refs[:count], refs[count : count + 3]
    sent, own, total = refs[count + 3 : -2], refs[-2], refs[-1]
    partial = spread(adjacency, blocks, total).astype(BF16)
    nodes = sent[0].shape[0]
    for step, out in enumerate(sent):
        out[...] = partial[step * nodes : (step + 1) * nodes]
    own[...] = dot(hidden[...], weight[...])


def last_kernel(count, *refs):
    got, (scale, own, weight, first, out) = refs[:count], refs[count:]

    @pl.when(lax.axis_index("layer") == 0)
    def _():
        out[...] = first[...]

    @pl.when(lax.axis_index("layer") != 0)
    def _():
        value = got[0][...].astype(F32)
        for part in got[1:]:
            value += part[...].astype(F32)
        inverse = jnp.concatenate([scale[...]] * (value.shape[1] // scale.shape[1]), axis=1)
        out[...] = (own[...] + dot((value * inverse).astype(BF16), weight[...])).astype(BF16)


def call(kernel, outs, specs, scratch=(), flops=0, moved=0):
    return pl.pallas_call(
        kernel,
        out_shape=outs,
        in_specs=specs,
        out_specs=jax.tree.map(lambda _: VMEM, outs),
        scratch_shapes=scratch,
        cost_estimate=pl.CostEstimate(flops=flops, bytes_accessed=moved, transcendentals=0),
    )


def body(
    sizes,
    features,
    class_ids,
    label_table,
    self_weight,
    neighbor_weight,
    norm_scale,
    tile_values,
    tile_block_row,
    tile_section,
    tile_count,
):
    layers, groups, splits = sizes
    nodes, width = features.shape
    edge = tile_values.shape[-1]
    direct = groups <= DIRECT
    rows = splits * edge
    shape = jax.ShapeDtypeStruct

    def index(layer, row, rep):
        return (layer * groups + row) * splits + rep

    def move(value, source, row_step, rep_step):
        pairs = []
        for row in range(groups):
            for rep in range(splits):
                target = index(1 - source, row ^ row_step, rep ^ rep_step)
                pairs.append((index(source, row, rep), target))
                pairs.append((index(1 - source, row, rep), index(source, row, rep)))
        return lax.ppermute(value, AXES, pairs)

    def over_rows(value, own):
        if direct:
            got = [move(value, 1, step, 0) for step in range(groups - 1, 0, -1)][::-1]
            return [move(value, 1, 0, 0) if own is None else own] + got
        value = move(value, 1, 0, 0) if own is None else own
        return [lax.all_gather(value, "row", axis=0, tiled=True)]

    def over_splits(parts):
        return [move(parts[step], 0, 0, step) for step in range(splits - 1, -1, -1)][::-1]

    x = call(embed_kernel, shape((nodes, width), BF16), [VMEM] * 3, moved=1)(
        class_ids.reshape(1, nodes), features, label_table
    )
    blocks = over_rows(x, x)
    chunk = groups if direct else CHUNK
    adjacency, degrees, own = call(
        functools.partial(build_kernel, direct),
        (
            shape((groups // chunk, rows, chunk * edge), BF16),
            shape((splits, PAD, width), BF16),
            shape((2 * nodes, width), BF16),
        ),
        [SMEM] * 3 + [VMEM] * 3,
        [pltpu.VMEM((groups, rows, edge), F32)],
        flops=10**8,
        moved=4 * 10**6,
    )(
        tile_block_row[0, 0],
        tile_section[0, 0],
        tile_count[0],
        tile_values[0, 0],
        x,
        self_weight[0],
    )
    room = [pltpu.VMEM((8, 128) if direct else (rows, width), F32)]
    count = len(blocks)
    sent = call(
        functools.partial(first_kernel, count),
        tuple(
            shape((nodes + PAD + (2 * nodes if step == 0 else 0), width), BF16)
            for step in range(splits)
        ),
        [VMEM] * (count + 4),
        room,
    )(*blocks, adjacency, degrees, own, neighbor_weight[0])
    hidden, scale = call(
        functools.partial(norm_kernel, splits),
        (shape((nodes, width), BF16), shape((nodes, nodes), F32)),
        [VMEM] * (splits + 1),
    )(*over_splits(sent), norm_scale.reshape(1, width))
    blocks = over_rows(hidden, None)
    first = blocks[0] if direct else move(hidden, 1, 0, 0)
    *sent, own = call(
        functools.partial(second_kernel, count),
        (shape((nodes, width), BF16),) * splits + (shape((nodes, width), F32),),
        [VMEM] * (count + 3),
        room,
    )(*blocks, adjacency, hidden, self_weight[0])
    out = call(
        functools.partial(last_kernel, splits),
        shape((nodes, width), BF16),
        [VMEM] * (splits + 4),
    )(*over_splits(sent), scale, own, neighbor_weight[0], first)
    return out[None]


def solution(mesh):
    sizes = tuple(mesh.shape[axis] for axis in AXES)
    return jax.shard_map(
        functools.partial(body, sizes),
        mesh=mesh,
        in_specs=(
            P(("row", "rep"), None),
            P(("row", "rep")),
            P(),
            P("layer", None, None),
            P("layer", None, None),
            P(),
            P("row", "rep", None, None, None),
            P("row", "rep", None),
            P("row", "rep", None),
            P("row", "rep"),
        ),
        out_specs=P("layer", ("row", "rep"), None),
        check_vma=False,
    )
```

```python
import functools

import jax
import jax.numpy as jnp
from jax import lax
from jax.experimental import pallas as pl
from jax.experimental.pallas import tpu as pltpu
from jax.sharding import PartitionSpec as P

AXES = ("layer", "row", "rep")
DIRECT = 8
CHUNK = 4
PAD = 16

VMEM = pl.BlockSpec(memory_space=pltpu.VMEM)
HBM = pl.BlockSpec(memory_space=pltpu.HBM)
SMEM = pl.BlockSpec(memory_space=pltpu.SMEM)
BF16 = jnp.bfloat16
F32 = jnp.float32


def in_hbm(value):
    return pltpu.with_memory_space_constraint(value, pltpu.HBM)


def dot(a, b, dims=((1,), (0,))):
    return lax.dot_general(a, b, (dims, ((), ())), preferred_element_type=F32)


def split(value):
    high = value.astype(BF16)
    return high, (value - high.astype(F32)).astype(BF16)


def fetch(pairs, semaphores):
    copies = [
        pltpu.make_async_copy(source, target, semaphores.at[number])
        for number, (source, target) in enumerate(pairs)
    ]
    for copy in copies:
        copy.start()
    return copies


def embed_kernel(ids_in, features_in, table_in, x, ids, features, table, semaphores):
    for copy in fetch([(ids_in, ids), (table_in, table), (features_in, features)], semaphores):
        copy.wait()
    classes, nodes = table.shape[0], features.shape[0]
    hot = (lax.broadcasted_iota(jnp.int32, (classes, nodes), 0) == ids[...]).astype(BF16)
    x[...] = (features[...].astype(F32) + dot(hot, table[...], ((0,), (0,)))).astype(BF16)


def build_kernel(
    direct,
    count,
    block_rows_in,
    sections_in,
    tiles_in,
    weight_in,
    x,
    adjacency,
    degrees,
    own,
    total,
    block_rows,
    sections,
    tiles,
    weight,
    semaphores,
):
    slots = tiles.shape[0]
    cut = slots // 2
    copies = fetch(
        [
            (block_rows_in, block_rows),
            (sections_in, sections),
            (tiles_in.at[0, 0, pl.ds(0, cut)], tiles.at[pl.ds(0, cut)]),
            (tiles_in.at[0, 0, pl.ds(cut, slots - cut)], tiles.at[pl.ds(cut, slots - cut)]),
            (weight_in, weight),
        ],
        semaphores,
    )
    row = lax.axis_index("row") if direct else 0
    rep = lax.axis_index("rep")
    edge = tiles.shape[1]
    splits = degrees.shape[0]
    total[...] = jnp.zeros_like(total)
    for copy in copies[:3]:
        copy.wait()

    def add(slot, carry):
        section = jnp.bitwise_xor(sections[0, 0, slot], row)
        start = pl.multiple_of(jnp.bitwise_xor(block_rows[0, 0, slot], rep) * edge, edge)
        total[section, pl.ds(start, edge), :] += tiles[slot].astype(F32)
        return carry

    used = count[0, 0]
    lax.fori_loop(0, jnp.minimum(used, cut), add, 0)
    for copy in copies[3:]:
        copy.wait()
    lax.fori_loop(cut, used, add, 0)
    chunks, rows, width = adjacency.shape
    per = width // edge
    ones = jnp.ones((PAD, width), BF16)

    def emit(chunk, sums):
        for part in range(per):
            adjacency[chunk, :, part * edge : (part + 1) * edge] = total[chunk * per + part].astype(BF16)
        return sums + dot(ones, adjacency[chunk], ((1,), (1,)))

    sums = jnp.zeros((PAD, rows), F32)
    if chunks == 1:
        sums = emit(0, sums)
    else:
        sums = lax.fori_loop(0, chunks, emit, sums)
    for step in range(splits):
        high, low = split(sums[:, step * edge : (step + 1) * edge])
        degrees[step, :, :edge] = high
        degrees[step, :, edge : 2 * edge] = low
    nodes = x.shape[0]
    high, low = split(dot(x[...], weight[0]))
    own[:nodes] = high
    own[nodes:] = low


def spread(adjacency, blocks, total):
    if len(blocks) > 1:
        return dot(adjacency[0], jnp.concatenate([block[...] for block in blocks], axis=0))
    chunks, _, width = adjacency.shape
    total[...] = jnp.zeros_like(total)

    def add(chunk, carry):
        start = pl.multiple_of(chunk * width, width)
        total[...] += dot(adjacency[chunk], blocks[0][pl.ds(start, width), :])
        return carry

    lax.fori_loop(0, chunks, add, 0)
    return total[...]


def first_kernel(count, *refs):
    blocks, (adjacency, degrees, own, weight) = refs[:count], refs[count : count + 4]
    sent, total = refs[count + 4 : -1], refs[-1]
    nodes = sent[1].shape[0] - PAD
    partial = spread(adjacency, blocks, total).astype(BF16)
    mixed = dot(partial, weight[...]).astype(BF16)
    for step, out in enumerate(sent):
        out[:nodes] = mixed[step * nodes : (step + 1) * nodes]
        out[nodes : nodes + PAD] = degrees[step]
    sent[0][nodes + PAD :] = own[...]


def norm_kernel(count, *refs):
    got, norm_scale = refs[:count], refs[count]
    hidden, scale = refs[count + 1 :]
    nodes = hidden.shape[0]
    value = got[0][:nodes].astype(F32)
    degree = got[0][nodes : nodes + PAD].astype(F32)
    for part in got[1:]:
        value += part[:nodes].astype(F32)
        degree += part[nodes : nodes + PAD].astype(F32)
    degree = degree[:1, :nodes] + degree[:1, nodes : 2 * nodes]
    diagonal = lax.broadcasted_iota(jnp.int32, (nodes, nodes), 0) == lax.broadcasted_iota(
        jnp.int32, (nodes, nodes), 1
    )
    inverse = jnp.sum(jnp.where(diagonal, lax.rsqrt(degree), 0.0), axis=1, keepdims=True)
    scale[...] = jnp.broadcast_to(inverse, scale.shape)
    own = got[0][nodes + PAD : 2 * nodes + PAD].astype(F32) + got[0][2 * nodes + PAD :].astype(F32)
    active = jnp.maximum(own + value * inverse, 0.0)
    center = active - jnp.mean(active, axis=-1, keepdims=True)
    spread_of = jnp.mean(center * center, axis=-1, keepdims=True)
    hidden[...] = (center * lax.rsqrt(spread_of + 1e-05) * norm_scale[...]).astype(BF16)


def second_kernel(count, *refs):
    blocks, (adjacency, hidden, weight) = refs[:count], refs[count : count + 3]
    sent, own, total = refs[count + 3 : -2], refs[-2], refs[-1]
    partial = spread(adjacency, blocks, total).astype(BF16)
    nodes = sent[0].shape[0]
    for step, out in enumerate(sent):
        out[...] = partial[step * nodes : (step + 1) * nodes]
    own[...] = dot(hidden[...], weight[...])


def last_kernel(count, *refs):
    got, (scale, own, weight, first, out) = refs[:count], refs[count:]

    @pl.when(lax.axis_index("layer") == 0)
    def _():
        out[...] = first[...]

    @pl.when(lax.axis_index("layer") != 0)
    def _():
        value = got[0][...].astype(F32)
        for part in got[1:]:
            value += part[...].astype(F32)
        inverse = jnp.concatenate([scale[...]] * (value.shape[1] // scale.shape[1]), axis=1)
        out[...] = (own[...] + dot((value * inverse).astype(BF16), weight[...])).astype(BF16)


def call(kernel, outs, specs, scratch=(), flops=0, moved=0, grant=16):
    return pl.pallas_call(
        kernel,
        out_shape=outs,
        in_specs=specs,
        out_specs=jax.tree.map(lambda _: VMEM, outs),
        scratch_shapes=scratch,
        compiler_params=pltpu.CompilerParams(vmem_limit_bytes=grant * 2**20),
        cost_estimate=pl.CostEstimate(flops=flops, bytes_accessed=moved, transcendentals=0),
    )


def body(
    sizes,
    features,
    class_ids,
    label_table,
    self_weight,
    neighbor_weight,
    norm_scale,
    tile_values,
    tile_block_row,
    tile_section,
    tile_count,
):
    layers, groups, splits = sizes
    nodes, width = features.shape
    edge = tile_values.shape[-1]
    direct = groups <= DIRECT
    rows = splits * edge
    shape = jax.ShapeDtypeStruct

    def index(layer, row, rep):
        return (layer * groups + row) * splits + rep

    def move(value, source, row_step, rep_step):
        pairs = []
        for row in range(groups):
            for rep in range(splits):
                target = index(1 - source, row ^ row_step, rep ^ rep_step)
                pairs.append((index(source, row, rep), target))
                pairs.append((index(1 - source, row, rep), index(source, row, rep)))
        return lax.ppermute(value, AXES, pairs)

    def over_rows(value, own):
        if direct:
            got = [move(value, 1, step, 0) for step in range(groups - 1, 0, -1)][::-1]
            return [move(value, 1, 0, 0) if own is None else own] + got
        value = move(value, 1, 0, 0) if own is None else own
        return [lax.all_gather(value, "row", axis=0, tiled=True)]

    def over_splits(parts):
        return [move(parts[step], 0, 0, step) for step in range(splits - 1, -1, -1)][::-1]

    x = call(
        embed_kernel,
        shape((nodes, width), BF16),
        [HBM] * 3,
        [
            pltpu.VMEM((1, nodes), jnp.int32),
            pltpu.VMEM(features.shape, BF16),
            pltpu.VMEM(label_table.shape, BF16),
            pltpu.SemaphoreType.DMA((3,)),
        ],
        moved=1,
    )(*map(in_hbm, (class_ids.reshape(1, nodes), features, label_table)))
    blocks = over_rows(x, x)
    chunk = groups if direct else CHUNK
    adjacency, degrees, own = call(
        functools.partial(build_kernel, direct),
        (
            shape((groups // chunk, rows, chunk * edge), BF16),
            shape((splits, PAD, width), BF16),
            shape((2 * nodes, width), BF16),
        ),
        [SMEM] + [HBM] * 4 + [VMEM],
        [
            pltpu.VMEM((groups, rows, edge), F32),
            pltpu.SMEM(tile_block_row.shape, jnp.int32),
            pltpu.SMEM(tile_section.shape, jnp.int32),
            pltpu.VMEM(tile_values.shape[2:], BF16),
            pltpu.VMEM(self_weight.shape, BF16),
            pltpu.SemaphoreType.DMA((5,)),
        ],
        flops=10**8,
        moved=4 * 10**6,
        grant=16 if direct else 48,
    )(
        tile_count,
        *map(in_hbm, (tile_block_row, tile_section, tile_values, self_weight)),
        x,
    )
    room = [pltpu.VMEM((8, 128) if direct else (rows, width), F32)]
    count = len(blocks)
    sent = call(
        functools.partial(first_kernel, count),
        tuple(
            shape((nodes + PAD + (2 * nodes if step == 0 else 0), width), BF16)
            for step in range(splits)
        ),
        [VMEM] * (count + 4),
        room,
    )(*blocks, adjacency, degrees, own, neighbor_weight[0])
    hidden, scale = call(
        functools.partial(norm_kernel, splits),
        (shape((nodes, width), BF16), shape((nodes, nodes), F32)),
        [VMEM] * (splits + 1),
    )(*over_splits(sent), norm_scale.reshape(1, width))
    blocks = over_rows(hidden, None)
    first = blocks[0] if direct else move(hidden, 1, 0, 0)
    *sent, own = call(
        functools.partial(second_kernel, count),
        (shape((nodes, width), BF16),) * splits + (shape((nodes, width), F32),),
        [VMEM] * (count + 3),
        room,
    )(*blocks, adjacency, hidden, self_weight[0])
    out = call(
        functools.partial(last_kernel, splits),
        shape((nodes, width), BF16),
        [VMEM] * (splits + 4),
    )(*over_splits(sent), scale, own, neighbor_weight[0], first)
    return out[None]


def solution(mesh):
    sizes = tuple(mesh.shape[axis] for axis in AXES)
    return jax.shard_map(
        functools.partial(body, sizes),
        mesh=mesh,
        in_specs=(
            P(("row", "rep"), None),
            P(("row", "rep")),
            P(),
            P("layer", None, None),
            P("layer", None, None),
            P(),
            P("row", "rep", None, None, None),
            P("row", "rep", None),
            P("row", "rep", None),
            P("row", "rep"),
        ),
        out_specs=P("layer", ("row", "rep"), None),
        check_vma=False,
    )
```
